32 devices in a mesh: prow: 8 (over z, y), pcol: 4 (over x, core).
Axes of the slice: x: 2, y: 2, z: 4, core: 2. Of those that a mesh axis runs over, the one named last changes fastest.
Arguments:
- ainv: bfloat16 [3, 8, 256, 6, 4, 256], P(None, 'prow', None, None, 'pcol'), may hold values from -0.078125 to 0.078125
- panel: bfloat16 [6, 4, 256, 1536], P(None, 'pcol', None, 'prow'), may hold values from -6 to 6
- structure: int32 [4, 24], replicated, may hold values 0 or 1
- widths: int32 [4], replicated, may hold values from 1 to 512, 1536 in all
Outputs:
- inverse_panel: bfloat16 [3, 8, 256, 1536], P(None, 'prow', None, 'pcol')
The draws below stay inside these ranges and needn't reach their ends.
Inputs may be any that keep to these rules, and one draw needn't show every extreme that they name: Supernode k owns the next widths[k] columns; the widths sum to 1536 and the widest is exactly 512.
All inputs are finite; a program needn't handle non-finite values.
Results may differ from the reference program's by a relative error of at most 0.001.
Values may be sent and summed in bfloat16 or wider, within the bound.
No kernel may reach another device: no remote copies, remote signals or barrier semaphores. Data moves between devices by JAX's collectives and lax.ppermute only.
A program may use at most 64 MiB of HBM per device.

```python
import math
import jax
import jax.numpy as jnp
import numpy as np
from jax import lax

B = 256
SUP = 4
WT = 1536
WMAX = 512
BR = 3
NB = 24
BC = 6
N_PROW = 8
N_PCOL = 4


def touch_ends(drawn, rng, least, largest):
    longest = drawn.shape.index(max(drawn.shape))
    spots = []
    for shift in (0, 1):
        where = [jax.random.randint(jax.random.fold_in(rng, axis), (), 0, length) for axis, length in enumerate(drawn.shape)]
        where[longest] = (where[longest] + shift) % drawn.shape[longest]
        spots.append(tuple(where))
    return drawn.at[spots[0]].set(least).at[spots[1]].set(largest)


def block_levels(rng, dims, split, least, high):
    gain, own = 1.0, jax.random.fold_in(rng, 6)
    for axis_at, blocks in split:
        steps = jnp.exp(jax.random.uniform(jax.random.fold_in(own, axis_at), (blocks,), jnp.float32, least / len(split), high / len(split)))
        gain = gain * jnp.repeat(steps, dims[axis_at] // blocks).reshape([-1 if axis == axis_at else 1 for axis in range(len(dims))])
    return gain


def split_up(count, total, most, slope):
    loads = [(1 << 20) // math.isqrt(rank ** slope) + 1 for rank in range(2, count + 1)]
    spare, holding = total - most - (count - 1), [1] * (count - 1)
    while spare > 0:
        movable = [i for i in range(count - 1) if holding[i] < most]
        pool, budget = sum([loads[i] for i in movable]), spare
        for i in movable:
            more = min(most - holding[i], max(1, budget * loads[i] // pool), spare)
            holding[i] = holding[i] + more
            spare = spare - more
    return np.array([most] + holding)


def uneven(key, amount, total, limit, slope):
    if amount == 2:
        one = jax.random.randint(key, (), max(1, total - limit), min(limit, total - 1) + 1)
        return jnp.stack([one, total - one])
    lengths = jnp.asarray(split_up(amount, total, limit, slope), jnp.int32)
    pairs = (amount - 1) // 2
    giver, receiver = lengths[1:1 + 2 * pairs:2], lengths[2:2 + 2 * pairs:2]
    slack = jnp.minimum(giver - 1, limit - receiver)
    moved = jax.random.randint(jax.random.fold_in(key, 1), (pairs,), 0, 1 << 20) % (slack + 1)
    lengths = lengths.at[1:1 + 2 * pairs:2].set(giver - moved).at[2:2 + 2 * pairs:2].set(receiver + moved)
    return lengths[jax.random.permutation(jax.random.fold_in(key, 2), amount)]


def noise(rng, dims, deviation, reach, split=(), kind=jnp.bfloat16):
    drawn = deviation * jax.random.normal(rng, dims, jnp.float32)
    if split:
        drawn = drawn * block_levels(rng, dims, split, -0.22, 0.18)
    return jnp.clip(drawn, -reach, reach).astype(kind)


def setup_inputs(seed: int = 0) -> dict:
    key_list = jax.random.split(jax.random.key(seed), 5)
    return {
        "ainv": noise(key_list[0], (BR, N_PROW, B, BC, N_PCOL, B), (NB * B) ** -0.5, 0.078125, ((1, 8), (4, 4))),
        "panel": noise(key_list[1], (BC, N_PCOL, B, WT), 1.0, 6.0, ((1, 4), (3, 8))),
        "structure": touch_ends((jax.random.randint(key_list[2], (SUP, NB), 0, 2) < 1).astype(jnp.int32), jax.random.fold_in(key_list[2], 1), 0, 1),
        "widths": uneven(key_list[3], SUP, WT, WMAX, 1).astype(jnp.int32),
    }


def owner_columns(widths, count):
    ends = jnp.cumsum(widths, dtype=jnp.int32)
    columns = jnp.arange(count, dtype=jnp.int32)
    return jnp.sum((columns[:, None] >= ends[None, :]).astype(jnp.int32), axis=1)


def reference(ainv, panel, structure, widths):
    blocks = structure.shape[1]
    order = blocks * B
    amat = ainv.reshape(order, order)
    pmat = panel.reshape(order, WT)
    owner = owner_columns(widths, WT)
    onehot = (owner[:, None] == jnp.arange(SUP, dtype=jnp.int32)[None, :]).astype(jnp.float32)
    block_keep = jnp.dot(structure.T.astype(jnp.float32), onehot.T, precision=lax.Precision.HIGHEST)
    keep = jnp.repeat(block_keep, B, axis=0)
    masked = (pmat.astype(jnp.float32) * keep).astype(jnp.bfloat16)
    product = jnp.dot(amat.astype(jnp.float32), masked.astype(jnp.float32), precision=lax.Precision.HIGHEST)
    result = (-(product * keep)).astype(jnp.bfloat16)
    return result.reshape(BR, N_PROW, B, WT)
```

```python
import functools

import jax
import jax.numpy as jnp
from jax import lax
from jax.experimental import pallas as pl
from jax.experimental.pallas import tpu as pltpu
from jax.sharding import PartitionSpec as P

SMEM = pl.BlockSpec(memory_space=pltpu.SMEM)


def column_onehot(widths, first, count, groups):
    ends = jnp.cumsum(widths, dtype=jnp.int32)
    columns = first + jnp.arange(count, dtype=jnp.int32)
    owner = jnp.sum((columns[:, None] >= ends[None, :]).astype(jnp.int32), axis=1)
    return (owner[:, None] == jnp.arange(groups, dtype=jnp.int32)[None, :]).astype(jnp.float32)


def plain_body(ainv, panel, structure, widths):
    rows_here, _, blk, cols_here, _, _ = ainv.shape
    groups = structure.shape[0]
    nprow = lax.axis_size("prow")
    npcol = lax.axis_size("pcol")
    row_id = lax.axis_index("prow")
    col_id = lax.axis_index("pcol")
    width_in = panel.shape[3]
    total = width_in * nprow
    width_out = total // npcol
    struct_float = structure.astype(jnp.float32)
    panel_struct = lax.dynamic_slice_in_dim(
        struct_float.reshape(groups, cols_here, npcol), col_id, 1, 2
    )[:, :, 0]
    onehot_in = column_onehot(widths, row_id * width_in, width_in, groups)
    keep_in = jnp.dot(panel_struct.T, onehot_in.T)
    masked = panel[:, 0] * keep_in[:, None, :].astype(jnp.bfloat16)
    amat = ainv.reshape(rows_here * blk, cols_here * blk)
    piece = lax.all_gather(masked, "prow", axis=2, tiled=True)
    partial_prod = jnp.dot(
        amat, piece.reshape(cols_here * blk, piece.shape[2]), preferred_element_type=jnp.float32
    )
    summed = lax.psum_scatter(partial_prod, "pcol", scatter_dimension=1, tiled=True)
    out_struct = lax.dynamic_slice_in_dim(
        struct_float.reshape(groups, rows_here, nprow), row_id, 1, 2
    )[:, :, 0]
    onehot_out = column_onehot(widths, col_id * width_out, width_out, groups)
    keep_out = jnp.dot(out_struct.T, onehot_out.T)
    result = -(summed.reshape(rows_here, blk, width_out) * keep_out[:, None, :])
    return result.astype(jnp.bfloat16).reshape(rows_here, 1, blk, width_out)


def ring_pos(row, n):
    return jnp.where(row % 2 == 0, row // 2, n - 1 - row // 2)


def ring_row(pos, n):
    return jnp.where(pos < n // 2, 2 * pos, 2 * (n - 1 - pos) + 1)


def owner_masks(widths_ref, first, rows, groups):
    cols = first + lax.broadcasted_iota(jnp.int32, (rows, 128), 0)
    masks, low = [], 0
    for k in range(groups):
        high = low + widths_ref[k]
        masks.append(((cols >= low) & (cols < high)).astype(jnp.float32))
        low = high
    return masks


def keep_of(masks, struct_ref, block):
    total = None
    for k, mask in enumerate(masks):
        term = mask * struct_ref[k, block].astype(jnp.float32)
        total = term if total is None else total + term
    return total


def multiply_kernel(offsets, n, npcol, width, struct_ref, widths_ref, *refs):
    count = len(offsets)
    panels, (own_ref, other_ref, send_ref, hold_ref, masked) = refs[: 2 * count], refs[2 * count :]
    depth, half, blk = panels[0].shape
    groups = struct_ref.shape[0]
    col = lax.axis_index("pcol")
    pos = ring_pos(lax.axis_index("prow"), n)

    @pl.when(pl.program_id(0) == 0)
    def _():
        for u, offset in enumerate(offsets):
            row = ring_row(lax.rem(pos + offset + n, n), n)
            masks = owner_masks(widths_ref, row * width + (col % 2) * half, half, groups)
            for q in range(2):
                part = col if q == 0 else col + 1 - 2 * (col % 2)
                for b in range(depth):
                    keep = keep_of(masks, struct_ref, b * npcol + part).astype(jnp.bfloat16)
                    for s in range(blk // 128):
                        at = pl.ds(s * 128, 128)
                        masked[q * depth + b, pl.ds(u * half, half), at] = (
                            panels[2 * u + q][b, :, at] * keep
                        )

    total = None
    for q, a_ref in enumerate((own_ref, other_ref)):
        for b in range(depth):
            term = lax.dot_general(
                masked[q * depth + b],
                a_ref[0, b],
                (((1,), (1,)), ((), ())),
                preferred_element_type=jnp.float32,
            )
            total = term if total is None else total + term
    first = (col // 2) == 0
    part = half // 2
    for u in range(count):
        low = total[u * half : u * half + part]
        high = total[u * half + part : (u + 1) * half]
        hold_ref[u] = jnp.where(first, low, high)
        send_ref[u] = jnp.where(first, high, low)


def multiply(offsets, n, npcol, width, structure, widths, panels, own, other):
    count = len(offsets)
    depth, half, blk = panels[0].shape
    rows = own.shape[0]
    shape = jax.ShapeDtypeStruct((count, half // 2, rows * blk), jnp.float32)
    whole = pl.BlockSpec((depth, half, blk), lambda a: (0, 0, 0))
    ablock = pl.BlockSpec((1, depth, blk, blk), lambda a: (a, 0, 0, 0))
    oblock = pl.BlockSpec((count, half // 2, blk), lambda a: (0, 0, a))
    flops = 2 * count * half * 2 * depth * blk * rows * blk
    return pl.pallas_call(
        functools.partial(multiply_kernel, offsets, n, npcol, width),
        grid=(rows,),
        in_specs=[SMEM, SMEM] + [whole] * (2 * count) + [ablock] * 2,
        out_specs=[oblock, oblock],
        out_shape=[shape, shape],
        scratch_shapes=[pltpu.VMEM((2 * depth, count * half, blk), jnp.bfloat16)],
        cost_estimate=pl.CostEstimate(
            flops=flops, bytes_accessed=4 * own.size + 4 * count * half * depth * blk, transcendentals=0
        ),
        name=f"multiply{count}",
    )(structure, widths, *panels, own, other)


def finish_kernel(offsets, n, width, struct_ref, widths_ref, hold_ref, got_ref, out_ref):
    count, part, height = hold_ref.shape
    groups = struct_ref.shape[0]
    me = lax.axis_index("prow")
    col = lax.axis_index("pcol")
    pos = ring_pos(me, n)
    blocks = struct_ref.shape[1] // n
    blk = height // blocks
    for u, offset in enumerate(offsets):
        row = ring_row(lax.rem(pos + offset + n, n), n)
        first = row * width + (col % 2) * 2 * part + (col // 2) * part
        masks = owner_masks(widths_ref, first, part, groups)
        for a in range(blocks):
            keep = keep_of(masks, struct_ref, a * n + me)
            for s in range(blk // 128):
                at = pl.ds(a * blk + s * 128, 128)
                value = -((hold_ref[u, :, at] + got_ref[u, :, at]) * keep)
                out_ref[u, :, at] = value.astype(jnp.bfloat16)


def finish(offsets, n, width, structure, widths, hold, got):
    whole = pl.BlockSpec(memory_space=pltpu.VMEM)
    return pl.pallas_call(
        functools.partial(finish_kernel, offsets, n, width),
        in_specs=[SMEM, SMEM, whole, whole],
        out_specs=whole,
        out_shape=jax.ShapeDtypeStruct(hold.shape, jnp.bfloat16),
        cost_estimate=pl.CostEstimate(flops=hold.size * 3, bytes_accessed=hold.size * 10, transcendentals=0),
        name="finish",
    )(structure, widths, hold, got)


def pick_kernel(offsets, n, *refs):
    parts, outs, store = refs[: len(offsets)], refs[len(offsets) : -1], refs[-1]
    col = lax.axis_index("pcol")
    pos = ring_pos(lax.axis_index("prow"), n)
    for ref, here in zip(parts, offsets):
        for u, offset in enumerate(here):
            store[offset % n] = ref[u]
    for j, out in enumerate(outs):
        to = col ^ j
        for y in range(2):
            out[y] = store[lax.rem(ring_pos(2 * to + y, n) - pos + n, n)]


def pick(offsets, n, npcol, parts):
    whole = pl.BlockSpec(memory_space=pltpu.VMEM)
    _, part, height = parts[0].shape
    shape = jax.ShapeDtypeStruct((n // npcol, part, height), jnp.bfloat16)
    return pl.pallas_call(
        functools.partial(pick_kernel, offsets, n),
        in_specs=[whole] * len(parts),
        out_specs=[whole] * npcol,
        out_shape=[shape] * npcol,
        scratch_shapes=[pltpu.VMEM((n, part, height), jnp.bfloat16)],
        name="pick",
    )(*parts)


def lay_kernel(width, *refs):
    parts, out_ref, store = refs[:-2], refs[-2], refs[-1]
    count, part, height = parts[0].shape
    col = lax.axis_index("pcol")
    for j, ref in enumerate(parts):
        source = col ^ j
        start = (source % 2) * 2 * part + (source // 2) * part
        for y in range(count):
            at = pl.multiple_of(y * width + start, 16)
            store[pl.ds(at, part), :] = ref[y].astype(jnp.float32)
    blocks, blk, columns = out_ref.shape
    for a in range(blocks):
        out_ref[a] = store[:, a * blk : (a + 1) * blk].T.astype(jnp.bfloat16)


def lay(width, blocks, parts):
    whole = pl.BlockSpec(memory_space=pltpu.VMEM)
    count, part, height = parts[0].shape
    columns = count * width
    return pl.pallas_call(
        functools.partial(lay_kernel, width),
        in_specs=[whole] * len(parts),
        out_specs=whole,
        out_shape=jax.ShapeDtypeStruct((blocks, height // blocks, columns), jnp.bfloat16),
        scratch_shapes=[pltpu.VMEM((columns, height), jnp.float32)],
        name="lay",
    )(*parts)


def ring_body(ainv, panel, structure, widths):
    n = lax.axis_size("prow")
    npcol = lax.axis_size("pcol")
    half_way = n // 2
    width = panel.shape[3]
    half = width // 2
    ring = list(range(0, n, 2)) + list(range(n - 1, 0, -2))
    up = [(ring[i], ring[(i + 1) % n]) for i in range(n)]
    down = [(ring[(i + 1) % n], ring[i]) for i in range(n)]
    side = [(c, c ^ 1) for c in range(npcol)]
    across = [(c, c ^ 2) for c in range(npcol)]
    core = lax.axis_index("pcol") % 2

    own = jnp.transpose(ainv, (0, 1, 3, 4, 2, 5))[:, 0, :, 0]
    cols = jnp.transpose(panel, (0, 1, 3, 2))[:, 0]
    mine = lax.dynamic_slice_in_dim(cols, core * half, half, 1)
    theirs = lax.dynamic_slice_in_dim(cols, (1 - core) * half, half, 1)
    a_up, a_down = [mine], [mine]
    a_up.append(lax.ppermute(mine, "prow", up))
    a_down.append(lax.ppermute(mine, "prow", down))
    partner = lax.ppermute(theirs, "pcol", side)
    b_up, b_down = [partner], [partner]
    other = lax.ppermute(own, "pcol", side)
    for s in range(1, half_way):
        b_up.append(lax.ppermute(b_up[-1], "prow", up))
        b_down.append(lax.ppermute(b_down[-1], "prow", down))
        if s + 1 < half_way:
            a_up.append(lax.ppermute(a_up[-1], "prow", up))
            a_down.append(lax.ppermute(a_down[-1], "prow", down))
    a_last = lax.ppermute(a_up[-1], "prow", up)
    b_last = lax.ppermute(b_down[-1], "prow", down)

    stages = [((0,), (mine, partner))]
    for s in range(1, half_way):
        stages.append(((-s, s), (a_up[s], b_up[s], a_down[s], b_down[s])))
    stages.append(((half_way,), (a_last, b_last)))

    done = []
    for offsets, panels in stages:
        send, hold = multiply(offsets, n, npcol, width, structure, widths, panels, own, other)
        got = lax.ppermute(send, "pcol", across)
        done.append(finish(offsets, n, width, structure, widths, hold, got))

    kept, *sends = pick([o for o, _ in stages], n, npcol, done)
    parts = [kept]
    for j, send in enumerate(sends, 1):
        parts.append(lax.ppermute(send, "pcol", [(c, c ^ j) for c in range(npcol)]))
    out = lay(width, own.shape[0], parts)
    return out[:, None]


def solution(mesh):
    in_specs = (P(None, "prow", None, None, "pcol", None), P(None, "pcol", None, "prow"), P(), P())
    out_specs = P(None, "prow", None, "pcol")
    n, npcol = mesh.shape["prow"], mesh.shape["pcol"]
    two_chips = npcol == 2 * 2 and n % 2 == 0 and n == 2 * npcol
    body = ring_body if two_chips else plain_body
    return jax.shard_map(body, mesh=mesh, in_specs=in_specs, out_specs=out_specs, check_vma=False)
```

```python
import functools

import jax
import jax.numpy as jnp
from jax import lax
from jax.experimental import pallas as pl
from jax.experimental.pallas import tpu as pltpu
from jax.sharding import PartitionSpec as P


SMEM = pl.BlockSpec(memory_space=pltpu.SMEM)


def column_onehot(widths, first, count, groups):
    ends = jnp.cumsum(widths, dtype=jnp.int32)
    columns = first + jnp.arange(count, dtype=jnp.int32)
    owner = jnp.sum((columns[:, None] >= ends[None, :]).astype(jnp.int32), axis=1)
    return (owner[:, None] == jnp.arange(groups, dtype=jnp.int32)[None, :]).astype(jnp.float32)


def plain_body(ainv, panel, structure, widths):
    rows_here, _, blk, cols_here, _, _ = ainv.shape
    groups = structure.shape[0]
    nprow = lax.axis_size("prow")
    npcol = lax.axis_size("pcol")
    row_id = lax.axis_index("prow")
    col_id = lax.axis_index("pcol")
    width_in = panel.shape[3]
    total = width_in * nprow
    width_out = total // npcol
    struct_float = structure.astype(jnp.float32)
    panel_struct = lax.dynamic_slice_in_dim(
        struct_float.reshape(groups, cols_here, npcol), col_id, 1, 2
    )[:, :, 0]
    onehot_in = column_onehot(widths, row_id * width_in, width_in, groups)
    keep_in = jnp.dot(panel_struct.T, onehot_in.T)
    masked = panel[:, 0] * keep_in[:, None, :].astype(jnp.bfloat16)
    amat = ainv.reshape(rows_here * blk, cols_here * blk)
    piece = lax.all_gather(masked, "prow", axis=2, tiled=True)
    partial_prod = jnp.dot(
        amat, piece.reshape(cols_here * blk, piece.shape[2]), preferred_element_type=jnp.float32
    )
    summed = lax.psum_scatter(partial_prod, "pcol", scatter_dimension=1, tiled=True)
    out_struct = lax.dynamic_slice_in_dim(
        struct_float.reshape(groups, rows_here, nprow), row_id, 1, 2
    )[:, :, 0]
    onehot_out = column_onehot(widths, col_id * width_out, width_out, groups)
    keep_out = jnp.dot(out_struct.T, onehot_out.T)
    result = -(summed.reshape(rows_here, blk, width_out) * keep_out[:, None, :])
    return result.astype(jnp.bfloat16).reshape(rows_here, 1, blk, width_out)


def ring_pos(row, n):
    return jnp.where(row % 2 == 0, row // 2, n - 1 - row // 2)


def ring_row(pos, n):
    return jnp.where(pos < n // 2, 2 * pos, 2 * (n - 1 - pos) + 1)


def owner_masks(widths_ref, first, rows, groups):
    cols = first + lax.broadcasted_iota(jnp.int32, (rows, 128), 0)
    masks, low = [], 0
    for k in range(groups):
        high = low + widths_ref[k]
        masks.append(((cols >= low) & (cols < high)).astype(jnp.float32))
        low = high
    return masks


def keep_of(masks, struct_ref, block):
    total = None
    for k, mask in enumerate(masks):
        term = mask * struct_ref[k, block].astype(jnp.float32)
        total = term if total is None else total + term
    return total


def multiply_kernel(offsets, n, npcol, width, struct_ref, widths_ref, *refs):
    count = len(offsets)
    panels, (own_ref, other_ref, send_ref, hold_ref, masked) = refs[: 2 * count], refs[2 * count :]
    depth, half, blk = panels[0].shape
    groups = struct_ref.shape[0]
    col = lax.axis_index("pcol")
    pos = ring_pos(lax.axis_index("prow"), n)

    @pl.when(pl.program_id(0) == 0)
    def _():
        for u, offset in enumerate(offsets):
            row = ring_row(lax.rem(pos + offset + n, n), n)
            masks = owner_masks(widths_ref, row * width + (col % 2) * half, half, groups)
            for q in range(2):
                part = col if q == 0 else col + 1 - 2 * (col % 2)
                for b in range(depth):
                    keep = keep_of(masks, struct_ref, b * npcol + part).astype(jnp.bfloat16)
                    for s in range(blk // 128):
                        at = pl.ds(s * 128, 128)
                        masked[q * depth + b, pl.ds(u * half, half), at] = (
                            panels[2 * u + q][b, :, at] * keep
                        )

    total = None
    for q, a_ref in enumerate((own_ref, other_ref)):
        for b in range(depth):
            term = lax.dot_general(
                masked[q * depth + b],
                a_ref[0, b],
                (((1,), (1,)), ((), ())),
                preferred_element_type=jnp.float32,
            )
            total = term if total is None else total + term
    first = (col // 2) == 0
    part = half // 2
    for u in range(count):
        low = total[u * half : u * half + part]
        high = total[u * half + part : (u + 1) * half]
        hold_ref[u] = jnp.where(first, low, high)
        send_ref[u] = jnp.where(first, high, low)


def multiply(offsets, n, npcol, width, structure, widths, panels, own, other):
    count = len(offsets)
    depth, half, blk = panels[0].shape
    rows = own.shape[0]
    shape = jax.ShapeDtypeStruct((count, half // 2, rows * blk), jnp.float32)
    whole = pl.BlockSpec((depth, half, blk), lambda a: (0, 0, 0))
    ablock = pl.BlockSpec((1, depth, blk, blk), lambda a: (a, 0, 0, 0))
    oblock = pl.BlockSpec((count, half // 2, blk), lambda a: (0, 0, a))
    flops = 2 * count * half * 2 * depth * blk * rows * blk
    return pl.pallas_call(
        functools.partial(multiply_kernel, offsets, n, npcol, width),
        grid=(rows,),
        in_specs=[SMEM, SMEM] + [whole] * (2 * count) + [ablock] * 2,
        out_specs=[oblock, oblock],
        out_shape=[shape, shape],
        scratch_shapes=[pltpu.VMEM((2 * depth, count * half, blk), jnp.bfloat16)],
        cost_estimate=pl.CostEstimate(
            flops=flops, bytes_accessed=4 * own.size + 4 * count * half * depth * blk, transcendentals=0
        ),
        compiler_params=pltpu.CompilerParams(vmem_limit_bytes=16 << 20),
    )(structure, widths, *panels, own, other)


def finish_kernel(offsets, n, width, struct_ref, widths_ref, hold_ref, got_ref, out_ref):
    _, part, height = hold_ref.shape
    groups = struct_ref.shape[0]
    me = lax.axis_index("prow")
    col = lax.axis_index("pcol")
    pos = ring_pos(me, n)
    blocks = struct_ref.shape[1] // n
    blk = height // blocks
    for u, offset in enumerate(offsets):
        row = ring_row(lax.rem(pos + offset + n, n), n)
        first = row * width + (col % 2) * 2 * part + (col // 2) * part
        masks = owner_masks(widths_ref, first, part, groups)
        for a in range(blocks):
            keep = keep_of(masks, struct_ref, a * n + me)
            for s in range(blk // 128):
                at = pl.ds(a * blk + s * 128, 128)
                value = -((hold_ref[u, :, at] + got_ref[u, :, at]) * keep)
                out_ref[u, :, at] = value.astype(jnp.bfloat16)


def finish(offsets, n, width, structure, widths, hold, got):
    whole = pl.BlockSpec(memory_space=pltpu.VMEM)
    return pl.pallas_call(
        functools.partial(finish_kernel, offsets, n, width),
        in_specs=[SMEM, SMEM, whole, whole],
        out_specs=whole,
        out_shape=jax.ShapeDtypeStruct(hold.shape, jnp.bfloat16),
        cost_estimate=pl.CostEstimate(flops=hold.size * 3, bytes_accessed=hold.size * 10, transcendentals=0),
        compiler_params=pltpu.CompilerParams(vmem_limit_bytes=4 << 20),
        name="finish",
    )(structure, widths, hold, got)


def pick_kernel(offsets, n, *refs):
    parts, outs, store = refs[: len(offsets)], refs[len(offsets) : -1], refs[-1]
    col = lax.axis_index("pcol")
    pos = ring_pos(lax.axis_index("prow"), n)
    for ref, here in zip(parts, offsets):
        for u, offset in enumerate(here):
            store[offset % n] = ref[u]
    for j, out in enumerate(outs):
        to = col ^ j
        for y in range(2):
            out[y] = store[lax.rem(ring_pos(2 * to + y, n) - pos + n, n)]


def pick(offsets, n, npcol, parts):
    whole = pl.BlockSpec(memory_space=pltpu.VMEM)
    _, part, height = parts[0].shape
    shape = jax.ShapeDtypeStruct((n // npcol, part, height), jnp.bfloat16)
    return pl.pallas_call(
        functools.partial(pick_kernel, offsets, n),
        in_specs=[whole] * len(parts),
        out_specs=[whole] * npcol,
        out_shape=[shape] * npcol,
        scratch_shapes=[pltpu.VMEM((n, part, height), jnp.bfloat16)],
        compiler_params=pltpu.CompilerParams(vmem_limit_bytes=6 << 20),
        name="pick",
    )(*parts)


def lay_kernel(width, *refs):
    parts, out_ref, store = refs[:-2], refs[-2], refs[-1]
    count, part, _ = parts[0].shape
    col = lax.axis_index("pcol")
    for j, ref in enumerate(parts):
        source = col ^ j
        start = (source % 2) * 2 * part + (source // 2) * part
        for y in range(count):
            at = pl.multiple_of(y * width + start, 16)
            store[pl.ds(at, part), :] = ref[y].astype(jnp.float32)
    blocks, blk, _ = out_ref.shape
    for a in range(blocks):
        out_ref[a] = store[:, a * blk : (a + 1) * blk].T.astype(jnp.bfloat16)


def lay(width, blocks, parts):
    whole = pl.BlockSpec(memory_space=pltpu.VMEM)
    count, _, height = parts[0].shape
    columns = count * width
    return pl.pallas_call(
        functools.partial(lay_kernel, width),
        in_specs=[whole] * len(parts),
        out_specs=whole,
        out_shape=jax.ShapeDtypeStruct((blocks, height // blocks, columns), jnp.bfloat16),
        scratch_shapes=[pltpu.VMEM((columns, height), jnp.float32)],
        compiler_params=pltpu.CompilerParams(vmem_limit_bytes=8 << 20),
        name="lay",
    )(*parts)


def ring_body(ainv, panel, structure, widths):
    n = lax.axis_size("prow")
    npcol = lax.axis_size("pcol")
    half_way = n // 2
    width = panel.shape[3]
    half = width // 2
    ring = list(range(0, n, 2)) + list(range(n - 1, 0, -2))
    up = [(ring[i], ring[(i + 1) % n]) for i in range(n)]
    down = [(ring[(i + 1) % n], ring[i]) for i in range(n)]
    side = [(c, c ^ 1) for c in range(npcol)]
    across = [(c, c ^ 2) for c in range(npcol)]
    core = lax.axis_index("pcol") % 2

    own = jnp.transpose(ainv, (0, 1, 3, 4, 2, 5))[:, 0, :, 0]
    cols = jnp.transpose(panel, (0, 1, 3, 2))[:, 0]
    mine = lax.dynamic_slice_in_dim(cols, core * half, half, 1)
    theirs = lax.dynamic_slice_in_dim(cols, (1 - core) * half, half, 1)
    partner = lax.ppermute(theirs, "pcol", side)
    other = lax.ppermute(own, "pcol", side)
    a_up, a_down, b_up, b_down = [mine], [mine], [partner], [partner]
    for _ in range(1, half_way):
        a_up.append(lax.ppermute(a_up[-1], "prow", up))
        a_down.append(lax.ppermute(a_down[-1], "prow", down))
        b_up.append(lax.ppermute(b_up[-1], "prow", up))
        b_down.append(lax.ppermute(b_down[-1], "prow", down))
    a_last = lax.ppermute(a_up[-1], "prow", up)
    b_last = lax.ppermute(b_down[-1], "prow", down)

    stages = [((0,), (mine, partner))]
    for s in range(1, half_way):
        stages.append(((-s, s), (a_up[s], b_up[s], a_down[s], b_down[s])))
    stages.append(((half_way,), (a_last, b_last)))

    done = []
    for offsets, panels in stages:
        send, hold = multiply(offsets, n, npcol, width, structure, widths, panels, own, other)
        got = lax.ppermute(send, "pcol", across)
        done.append(finish(offsets, n, width, structure, widths, hold, got))

    kept, *sends = pick([o for o, _ in stages], n, npcol, done)
    parts = [kept]
    for j, send in enumerate(sends, 1):
        parts.append(lax.ppermute(send, "pcol", [(c, c ^ j) for c in range(npcol)]))
    out = lay(width, own.shape[0], parts)
    return out[:, None]


def solution(mesh):
    in_specs = (P(None, "prow", None, None, "pcol", None), P(None, "pcol", None, "prow"), P(), P())
    out_specs = P(None, "prow", None, "pcol")
    n, npcol = mesh.shape["prow"], mesh.shape["pcol"]
    two_chips = npcol == 2 * 2 and n % 2 == 0 and n == 2 * npcol
    if not two_chips:
        return jax.shard_map(plain_body, mesh=mesh, in_specs=in_specs, out_specs=out_specs, check_vma=False)
    return jax.shard_map(
        ring_body, mesh=mesh, in_specs=in_specs, out_specs=out_specs, check_vma=False
    )
```

```python
import functools

import jax
import jax.numpy as jnp
from jax import lax
from jax.experimental import pallas as pl
from jax.experimental.pallas import tpu as pltpu
from jax.sharding import PartitionSpec as P


SMEM = pl.BlockSpec(memory_space=pltpu.SMEM)


def column_onehot(widths, first, count, groups):
    ends = jnp.cumsum(widths, dtype=jnp.int32)
    columns = first + jnp.arange(count, dtype=jnp.int32)
    owner = jnp.sum((columns[:, None] >= ends[None, :]).astype(jnp.int32), axis=1)
    return (owner[:, None] == jnp.arange(groups, dtype=jnp.int32)[None, :]).astype(jnp.float32)


def plain_body(ainv, panel, structure, widths):
    rows_here, _, blk, cols_here, _, _ = ainv.shape
    groups = structure.shape[0]
    nprow = lax.axis_size("prow")
    npcol = lax.axis_size("pcol")
    row_id = lax.axis_index("prow")
    col_id = lax.axis_index("pcol")
    width_in = panel.shape[3]
    total = width_in * nprow
    width_out = total // npcol
    struct_float = structure.astype(jnp.float32)
    panel_struct = lax.dynamic_slice_in_dim(
        struct_float.reshape(groups, cols_here, npcol), col_id, 1, 2
    )[:, :, 0]
    onehot_in = column_onehot(widths, row_id * width_in, width_in, groups)
    keep_in = jnp.dot(panel_struct.T, onehot_in.T)
    masked = panel[:, 0] * keep_in[:, None, :].astype(jnp.bfloat16)
    amat = ainv.reshape(rows_here * blk, cols_here * blk)
    piece = lax.all_gather(masked, "prow", axis=2, tiled=True)
    partial_prod = jnp.dot(
        amat, piece.reshape(cols_here * blk, piece.shape[2]), preferred_element_type=jnp.float32
    )
    summed = lax.psum_scatter(partial_prod, "pcol", scatter_dimension=1, tiled=True)
    out_struct = lax.dynamic_slice_in_dim(
        struct_float.reshape(groups, rows_here, nprow), row_id, 1, 2
    )[:, :, 0]
    onehot_out = column_onehot(widths, col_id * width_out, width_out, groups)
    keep_out = jnp.dot(out_struct.T, onehot_out.T)
    result = -(summed.reshape(rows_here, blk, width_out) * keep_out[:, None, :])
    return result.astype(jnp.bfloat16).reshape(rows_here, 1, blk, width_out)


def ring_pos(row, n):
    return jnp.where(row % 2 == 0, row // 2, n - 1 - row // 2)


def ring_row(pos, n):
    return jnp.where(pos < n // 2, 2 * pos, 2 * (n - 1 - pos) + 1)


def owner_masks(widths_ref, first, rows, groups):
    cols = first + lax.broadcasted_iota(jnp.int32, (rows, 128), 0)
    masks, low = [], 0
    for k in range(groups):
        high = low + widths_ref[k]
        masks.append(((cols >= low) & (cols < high)).astype(jnp.float32))
        low = high
    return masks


def keep_of(masks, struct_ref, block):
    total = None
    for k, mask in enumerate(masks):
        term = mask * struct_ref[k, block].astype(jnp.float32)
        total = term if total is None else total + term
    return total


def multiply_kernel(offsets, n, npcol, width, struct_ref, widths_ref, *refs):
    count = len(offsets)
    panels, (own_ref, other_ref, send_ref, hold_ref, masked) = refs[: 2 * count], refs[2 * count :]
    depth, half, blk = panels[0].shape
    groups = struct_ref.shape[0]
    col = lax.axis_index("pcol")
    pos = ring_pos(lax.axis_index("prow"), n)

    for u, offset in enumerate(offsets):
        row = ring_row(lax.rem(pos + offset + n, n), n)
        masks = owner_masks(widths_ref, row * width + (col % 2) * half, half, groups)
        for q in range(2):
            part = col if q == 0 else col + 1 - 2 * (col % 2)
            for b in range(depth):
                keep = keep_of(masks, struct_ref, b * npcol + part).astype(jnp.bfloat16)
                for s in range(blk // 128):
                    at = pl.ds(s * 128, 128)
                    masked[q * depth + b, pl.ds(u * half, half), at] = (
                        panels[2 * u + q][b, :, at] * keep
                    )

    first = (col // 2) == 0
    part = half // 2
    for a in range(own_ref.shape[0]):
        total = None
        for q, a_ref in enumerate((own_ref, other_ref)):
            for b in range(depth):
                term = lax.dot_general(
                    masked[q * depth + b],
                    a_ref[a, b],
                    (((1,), (1,)), ((), ())),
                    preferred_element_type=jnp.float32,
                )
                total = term if total is None else total + term
        at = pl.ds(a * blk, blk)
        for u in range(count):
            low = total[u * half : u * half + part]
            high = total[u * half + part : (u + 1) * half]
            hold_ref[u, :, at] = jnp.where(first, low, high)
            send_ref[u, :, at] = jnp.where(first, high, low)


def multiply(offsets, n, npcol, width, structure, widths, panels, own, other):
    count = len(offsets)
    depth, half, blk = panels[0].shape
    rows = own.shape[0]
    shape = jax.ShapeDtypeStruct((count, half // 2, rows * blk), jnp.float32)
    whole = pl.BlockSpec(memory_space=pltpu.VMEM)
    flops = 2 * count * half * 2 * depth * blk * rows * blk
    return pl.pallas_call(
        functools.partial(multiply_kernel, offsets, n, npcol, width),
        in_specs=[SMEM, SMEM] + [whole] * (2 * count + 2),
        out_specs=[whole, whole],
        out_shape=[shape, shape],
        scratch_shapes=[pltpu.VMEM((2 * depth, count * half, blk), jnp.bfloat16)],
        cost_estimate=pl.CostEstimate(
            flops=flops, bytes_accessed=4 * own.size + 4 * count * half * depth * blk, transcendentals=0
        ),
        compiler_params=pltpu.CompilerParams(vmem_limit_bytes=16 << 20),
    )(structure, widths, *panels, own, other)


def finish_kernel(offsets, n, width, struct_ref, widths_ref, hold_ref, got_ref, out_ref):
    _, part, height = hold_ref.shape
    groups = struct_ref.shape[0]
    me = lax.axis_index("prow")
    col = lax.axis_index("pcol")
    pos = ring_pos(me, n)
    blocks = struct_ref.shape[1] // n
    blk = height // blocks
    for u, offset in enumerate(offsets):
        row = ring_row(lax.rem(pos + offset + n, n), n)
        first = row * width + (col % 2) * 2 * part + (col // 2) * part
        masks = owner_masks(widths_ref, first, part, groups)
        for a in range(blocks):
            keep = keep_of(masks, struct_ref, a * n + me)
            for s in range(blk // 128):
                at = pl.ds(a * blk + s * 128, 128)
                value = -((hold_ref[u, :, at] + got_ref[u, :, at]) * keep)
                out_ref[u, :, at] = value.astype(jnp.bfloat16)


def finish(offsets, n, width, structure, widths, hold, got):
    whole = pl.BlockSpec(memory_space=pltpu.VMEM)
    return pl.pallas_call(
        functools.partial(finish_kernel, offsets, n, width),
        in_specs=[SMEM, SMEM, whole, whole],
        out_specs=whole,
        out_shape=jax.ShapeDtypeStruct(hold.shape, jnp.bfloat16),
        cost_estimate=pl.CostEstimate(flops=hold.size * 3, bytes_accessed=hold.size * 10, transcendentals=0),
        compiler_params=pltpu.CompilerParams(vmem_limit_bytes=4 << 20),
        name="finish",
    )(structure, widths, hold, got)


def pick_kernel(offsets, n, *refs):
    parts, outs, store = refs[: len(offsets)], refs[len(offsets) : -1], refs[-1]
    col = lax.axis_index("pcol")
    pos = ring_pos(lax.axis_index("prow"), n)
    for ref, here in zip(parts, offsets):
        for u, offset in enumerate(here):
            store[offset % n] = ref[u]
    for j, out in enumerate(outs):
        to = col ^ j
        for y in range(2):
            out[y] = store[lax.rem(ring_pos(2 * to + y, n) - pos + n, n)]


def pick(offsets, n, npcol, parts):
    whole = pl.BlockSpec(memory_space=pltpu.VMEM)
    _, part, height = parts[0].shape
    shape = jax.ShapeDtypeStruct((n // npcol, part, height), jnp.bfloat16)
    return pl.pallas_call(
        functools.partial(pick_kernel, offsets, n),
        in_specs=[whole] * len(parts),
        out_specs=[whole] * npcol,
        out_shape=[shape] * npcol,
        scratch_shapes=[pltpu.VMEM((n, part, height), jnp.bfloat16)],
        compiler_params=pltpu.CompilerParams(vmem_limit_bytes=6 << 20),
        name="pick",
    )(*parts)


def lay_kernel(n, width, *refs):
    parts, out_ref, store = refs[:-2], refs[-2], refs[-1]
    early, last = parts[: len(parts) // 2], parts[len(parts) // 2 :]
    count, part, _ = early[0].shape
    col = lax.axis_index("pcol")
    pos = ring_pos(lax.axis_index("prow"), n)
    for j, (ref, end) in enumerate(zip(early, last)):
        source = col ^ j
        start = (source % 2) * 2 * part + (source // 2) * part
        for y in range(count):
            at = pl.multiple_of(y * width + start, 16)
            is_last = lax.rem(ring_pos(2 * col + y, n) - pos + n, n) == n // 2
            value = jnp.where(is_last, end[0].astype(jnp.float32), ref[y].astype(jnp.float32))
            store[pl.ds(at, part), :] = value
    blocks, blk, _ = out_ref.shape
    for a in range(blocks):
        out_ref[a] = store[:, a * blk : (a + 1) * blk].T.astype(jnp.bfloat16)


def lay(n, width, blocks, early, last):
    whole = pl.BlockSpec(memory_space=pltpu.VMEM)
    count, _, height = early[0].shape
    columns = count * width
    return pl.pallas_call(
        functools.partial(lay_kernel, n, width),
        in_specs=[whole] * (len(early) + len(last)),
        out_specs=whole,
        out_shape=jax.ShapeDtypeStruct((blocks, height // blocks, columns), jnp.bfloat16),
        scratch_shapes=[pltpu.VMEM((columns, height), jnp.float32)],
        compiler_params=pltpu.CompilerParams(vmem_limit_bytes=8 << 20),
        name="lay",
    )(*early, *last)


def ring_body(ainv, panel, structure, widths):
    n = lax.axis_size("prow")
    npcol = lax.axis_size("pcol")
    half_way = n // 2
    width = panel.shape[3]
    half = width // 2
    ring = list(range(0, n, 2)) + list(range(n - 1, 0, -2))
    up = [(ring[i], ring[(i + 1) % n]) for i in range(n)]
    down = [(ring[(i + 1) % n], ring[i]) for i in range(n)]
    side = [(c, c ^ 1) for c in range(npcol)]
    across = [(c, c ^ 2) for c in range(npcol)]
    core = lax.axis_index("pcol") % 2

    own = jnp.transpose(ainv, (0, 1, 3, 4, 2, 5))[:, 0, :, 0]
    cols = jnp.transpose(panel, (0, 1, 3, 2))[:, 0]
    mine = lax.dynamic_slice_in_dim(cols, core * half, half, 1)
    later, _ = lax.optimization_barrier((cols, mine))
    theirs = lax.dynamic_slice_in_dim(later, (1 - core) * half, half, 1)
    partner = lax.ppermute(theirs, "pcol", side)
    other = lax.ppermute(own, "pcol", side)
    a_up, a_down, b_up, b_down = [mine], [mine], [partner], [partner]
    for _ in range(1, half_way):
        a_up.append(lax.ppermute(a_up[-1], "prow", up))
        a_down.append(lax.ppermute(a_down[-1], "prow", down))
        b_up.append(lax.ppermute(b_up[-1], "prow", up))
        b_down.append(lax.ppermute(b_down[-1], "prow", down))
    a_last = lax.ppermute(a_up[-1], "prow", up)
    b_last = lax.ppermute(b_down[-1], "prow", down)

    stages = [((0,), (mine, partner))]
    for s in range(1, half_way):
        stages.append(((-s, s), (a_up[s], b_up[s], a_down[s], b_down[s])))
    stages.append(((half_way,), (a_last, b_last)))

    done = []
    for offsets, panels in stages:
        send, hold = multiply(offsets, n, npcol, width, structure, widths, panels, own, other)
        got = lax.ppermute(send, "pcol", across)
        done.append(finish(offsets, n, width, structure, widths, hold, got))

    kept, *sends = pick([o for o, _ in stages[:-1]], n, npcol, done[:-1])
    early, last = [kept], [done[-1]]
    for j, send in enumerate(sends, 1):
        early.append(lax.ppermute(send, "pcol", [(c, c ^ j) for c in range(npcol)]))
    for j in range(1, npcol):
        ends = [(r, ring[(ring.index(r) + half_way) % n] // 2) for r in range(n)]
        perm = [(r * npcol + (to ^ j), r * npcol + to) for r, to in ends]
        last.append(lax.ppermute(done[-1], ("prow", "pcol"), perm))
    out = lay(n, width, own.shape[0], early, last)
    return out[:, None]


def solution(mesh):
    in_specs = (P(None, "prow", None, None, "pcol", None), P(None, "pcol", None, "prow"), P(), P())
    out_specs = P(None, "prow", None, "pcol")
    n, npcol = mesh.shape["prow"], mesh.shape["pcol"]
    two_chips = npcol == 2 * 2 and n % 2 == 0 and n == 2 * npcol
    if not two_chips:
        return jax.shard_map(plain_body, mesh=mesh, in_specs=in_specs, out_specs=out_specs, check_vma=False)
    return jax.shard_map(
        ring_body, mesh=mesh, in_specs=in_specs, out_specs=out_specs, check_vma=False
    )
```
